32 devices in a mesh: row: 4 (over z), col: 8 (over y, x, core).
Axes of the slice: x: 2, y: 2, z: 4, core: 2. Of those that a mesh axis runs over, the one named last changes fastest.
Arguments:
- trace: float32 [16, 4, 8, 8, 128, 128], P(None, 'row', None, 'col'), may hold values from -6 to 6
- fill: int32 [16, 4, 8, 8], P(None, 'row', None, 'col'), may hold values 0 or 1
- pivots: float32 [2, 128, 128], replicated, may hold values from -0.046875 to 0.046875
- direct_rhs: float32 [16, 4, 16, 128], P(None, 'row'), may hold values from -6 to 6
- adjoint_rhs: float32 [16, 4, 16, 128], P(None, 'row'), may hold values from -6 to 6
Outputs:
- factored: float32 [16, 4, 8, 8, 128, 128], P(None, 'row', None, 'col')
- direct: float32 [16, 4, 16, 128], P(None, 'row')
- adjoint: float32 [16, 4, 16, 128], P(None, 'row')
- image: float32 [16, 4, 16, 128], P(None, 'row', 'col')
- back_image: float32 [8, 8, 16, 128], P(None, 'col', 'row')
The draws below stay inside these ranges and needn't reach their ends.
All inputs are finite; a program needn't handle non-finite values. No bound on the sum of `fill` on one device may be relied on, other than what follows from the above.
Results may differ from the reference program's by a relative error of at most 0.0003.
Values sent between devices are 32-bit elements; how exact they have to be, the bound alone decides.
A program may use at most 128 MiB of HBM per device.

```python
import jax
import jax.numpy as jnp
from jax import lax

BLOCK = 128
RB = 16
MODES = 16
CB = 8
NB = 64
N_ROW = 4
N_COL = 8


def set_ends(entries, key, least, top_value):
    longest = entries.shape.index(max(entries.shape))
    spots = []
    for shift in (0, 1):
        where = [jax.random.randint(jax.random.fold_in(key, axis), (), 0, length) for axis, length in enumerate(entries.shape)]
        where[longest] = (where[longest] + shift) % entries.shape[longest]
        spots.append(tuple(where))
    return entries.at[spots[0]].set(least).at[spots[1]].set(top_value)


def block_levels(rng, shape, cuts, smallest, largest):
    gain = 1.0
    for dim, blocks in cuts:
        draws = jax.random.uniform(jax.random.fold_in(jax.random.fold_in(rng, 6), dim), (blocks,), jnp.float32, smallest / len(cuts), largest / len(cuts))
        gain = gain * jnp.repeat(jnp.exp(draws), shape[dim] // blocks).reshape((-1,) + (1,) * (len(shape) - 1 - dim))
    return gain


def normal_values(rng, shape, deviation, bound, cuts=(), kind=jnp.bfloat16):
    entries = jax.random.normal(rng, shape, jnp.float32) * deviation
    if len(cuts) > 0:
        entries = block_levels(rng, shape, cuts, -0.22, 0.18) * entries
    return jnp.clip(entries, min=-bound, max=bound).astype(kind)


def setup_inputs(seed: int = 0) -> dict:
    key_of = jax.random.split(jax.random.key(seed), 6)
    return {
        "trace": normal_values(key_of[0], (RB, N_ROW, CB, N_COL, BLOCK, BLOCK), 1.0, 6.0, ((1, 4), (3, 8)), jnp.float32),
        "fill": set_ends((jax.random.randint(key_of[1], (RB, N_ROW, CB, N_COL), 0, 4) < 3).astype(jnp.int32), jax.random.fold_in(key_of[1], 1), 0, 1),
        "pivots": normal_values(key_of[2], (2, BLOCK, BLOCK), (BLOCK * BLOCK) ** -0.5, 0.046875, (), jnp.float32),
        "direct_rhs": normal_values(key_of[3], (RB, N_ROW, MODES, BLOCK), 1.0, 6.0, ((1, 4),), jnp.float32),
        "adjoint_rhs": normal_values(key_of[4], (RB, N_ROW, MODES, BLOCK), 1.0, 6.0, ((1, 4),), jnp.float32),
    }


def reference(trace, fill, pivots, direct_rhs, adjoint_rhs):
    highest = lax.Precision.HIGHEST
    blocks = (trace * fill[:, :, :, :, None, None].astype(jnp.float32)).reshape(NB, NB, BLOCK, BLOCK)
    order = jnp.arange(NB)
    for panel in range(2):
        below = order > panel
        formed = jnp.einsum('iab,bc->iac', blocks[:, panel], pivots[panel], precision=highest)
        lower = jnp.where(below[:, None, None], formed, blocks[:, panel])
        upper = blocks[panel]

        def update_row(item, upper=upper, panel=panel):
            row_blocks, lower_block, flag = item
            change = jnp.einsum('ab,jbc->jac', lower_block, upper, precision=highest)
            keep = (flag & (order > panel))[:, None, None]
            row_blocks = row_blocks - jnp.where(keep, change, 0.0)
            return row_blocks.at[panel].set(lower_block)

        blocks = lax.map(update_row, (blocks, lower, below))
    solution = direct_rhs.reshape(NB, MODES, BLOCK)
    for panel in range(2):
        column = jnp.where((order > panel)[:, None, None], blocks[:, panel], 0.0)
        solution = solution - jnp.einsum('iab,mb->ima', column, solution[panel], precision=highest)
    adjoint = adjoint_rhs.reshape(NB, MODES, BLOCK)
    for panel in (1, 0):
        column = jnp.where((order > panel)[:, None, None], blocks[:, panel], 0.0)
        adjoint = adjoint.at[panel].add(-jnp.einsum('iab,ima->mb', column, adjoint, precision=highest))
    scale = (NB * BLOCK) ** -0.5
    image = jnp.einsum('ijab,jmb->ima', blocks, solution, precision=highest) * scale
    back = jnp.einsum('ijab,ima->jmb', blocks, adjoint, precision=highest) * scale
    return (blocks.reshape(RB, N_ROW, CB, N_COL, BLOCK, BLOCK),
            solution.reshape(RB, N_ROW, MODES, BLOCK),
            adjoint.reshape(RB, N_ROW, MODES, BLOCK),
            image.reshape(RB, N_ROW, MODES, BLOCK),
            back.reshape(CB, N_COL, MODES, BLOCK))
```

```python
import functools

import jax
import jax.numpy as jnp
from jax import lax
from jax.experimental import pallas as pl
from jax.experimental.pallas import tpu as pltpu
from jax.sharding import PartitionSpec as P

F32 = jnp.float32
BF16 = jnp.bfloat16
NN = (((1,), (0,)), ((), ()))
NT = (((1,), (1,)), ((), ()))


def split(x):
    high = x.astype(BF16)
    return high, (x - high.astype(F32)).astype(BF16)


def mul(a, b, dims):
    return lax.dot_general(a, b, dims, preferred_element_type=F32)


def dot3(a, b, dims):
    ah, al = split(a)
    bh, bl = split(b)
    return mul(ah, bh, dims) + mul(ah, bl, dims) + mul(al, bh, dims)


def stack(x):
    high, low = split(x)
    return jnp.concatenate([high, low], axis=0)


def thin(pair, bh, bl, dims):
    half = pair.shape[0] // 2
    both = mul(pair, bh, dims)
    return both[:half] + both[half:] + mul(pair[:half], bl, dims)


def comm_kernel(
    n_row, n_col, fill, piv, direct_rhs, adjoint_rhs, trace,
    fcol, upper, y_out, z_out, image, back,
    colbuf, rowbuf, mbuf, small, wloc, wrecv, ysel, ypair, zpair,
    img_p, img_t, img_r, back_p, back_t, back_r,
    load_sem, m_sem, sm_send, sm_recv, ring_send, ring_recv, sib_send, sib_recv,
    row_up, row_down, row_recv, w_send, w_recv, y_send, y_recv,
    is_send, is_recv, bs_send, bs_recv,
):
    rows, cols = mbuf.shape[0], mbuf.shape[1]
    modes = y_out.shape[1]
    width = y_out.shape[2]
    img_modes, back_modes = modes // n_col, modes // n_row
    scale = (rows * n_row * width) ** (-0.5)
    p = lax.axis_index("row")
    q = lax.axis_index("col")
    chips = n_col // 2
    deep = chips // 2
    chip, core = q // 2, q % 2
    cy, cx = chip // 2, chip % 2
    pos = cx * (cy + 1) + (1 - cx) * ((chips - cy) % chips)

    def at_pos(r):
        side = 1 - ((r + chips - 1) % chips) // deep
        return (side * ((r - 1) * 2 + 1) + (1 - side) * (((chips - r) % chips) * 2)) * 2 + core

    after = at_pos((pos + 1) % chips)
    before = at_pos((pos + chips - 1) % chips)
    sibling = chip * 2 + 1 - core
    half = rows // 2

    def to(src, dst, send, recv, row, col):
        return pltpu.make_async_remote_copy(
            src_ref=src, dst_ref=dst, send_sem=send, recv_sem=recv,
            device_id=(row, col), device_id_type=pl.DeviceIdType.MESH,
        )

    col_load = pltpu.make_async_copy(trace.at[:, 0], colbuf.at[core, pl.ds(0, rows)], load_sem.at[0])
    row_load = pltpu.make_async_copy(trace.at[0], rowbuf.at[lax.rem(p, 2)], load_sem.at[1])

    @pl.when(q < 2)
    def _():
        col_load.start()

    @pl.when(p < 2)
    def _():
        row_load.start()

    m_load = pltpu.make_async_copy(trace, mbuf, m_sem)
    m_load.start()

    barrier = pltpu.get_barrier_semaphore()
    for d in range(1, n_col):
        pl.semaphore_signal(barrier, inc=1, device_id=(p, (q + d) % n_col), device_id_type=pl.DeviceIdType.MESH)
    for d in range(1, n_row):
        pl.semaphore_signal(barrier, inc=1, device_id=((p + d) % n_row, q), device_id_type=pl.DeviceIdType.MESH)

    @pl.when(q < 2)
    def _():
        col_load.wait()

        def mask(a, _):
            colbuf[core, a] = colbuf[core, a] * fill[a, 0].astype(F32)
            return 0

        lax.fori_loop(0, rows, mask, 0)

    @pl.when(p < 2)
    def _():
        row_load.wait()
        slot = lax.rem(p, 2)

        def mask(c, _):
            rowbuf[slot, c] = rowbuf[slot, c] * fill[0, c].astype(F32)
            return 0

        lax.fori_loop(0, cols, mask, 0)
        small[slot, 0] = direct_rhs[0]
        small[slot, 1] = adjoint_rhs[0]

    pl.semaphore_wait(barrier, n_col + n_row - 2)

    def small_copy(kind, d):
        src = (direct_rhs, adjoint_rhs)[kind].at[0]
        return to(src, small.at[lax.rem(p, 2), kind], sm_send.at[kind, d], sm_recv.at[lax.rem(p, 2), kind], (p + d) % n_row, q)

    def ring(block, dest):
        ref = colbuf.at[core, block]
        return to(ref, ref, ring_send.at[block], ring_recv.at[block], p, dest)

    def sib(block, which):
        ref = colbuf.at[which, block]
        return to(ref, ref, sib_send.at[block], sib_recv.at[block], p, sibling)

    def row_copy(k, c, upward):
        ref = rowbuf.at[k, c]
        sems = row_up if upward else row_down
        dest = lax.rem(p + (1 if upward else n_row - 1), n_row)
        return to(ref, ref, sems.at[k, c], row_recv.at[k, c], dest, q)

    @pl.when(pos == 0)
    def _():
        def send(s, _):
            ring(s, after).start()
            ring(half + s, before).start()
            return 0

        lax.fori_loop(0, half, send, 0)

    for k in range(2):
        @pl.when(p == k)
        def _(k=k):
            def send(c, _):
                if k + 1 < n_row:
                    row_copy(k, c, True).start()
                if k > 0:
                    row_copy(k, c, False).start()
                return 0

            lax.fori_loop(0, cols, send, 0)

    @pl.when(p < 2)
    def _():
        for d in range(1, n_row):
            for kind in range(2):
                small_copy(kind, d).start()

    @pl.when(pos == 0)
    def _():
        def send(s, _):
            sib(s, core).start()
            return 0

        lax.fori_loop(0, rows, send, 0)

    def ring_step(block, forward):
        @pl.when(pos != 0)
        def _():
            dest = after if forward else before
            ring(block, dest).wait_recv()
            stop = chips - 1 if forward else 1

            @pl.when(pos != stop)
            def _():
                ring(block, dest).start()

            sib(block, core).start()

    def row_step(c):
        for k in range(2):
            @pl.when(p != k)
            def _(k=k):
                row_copy(k, c, True).wait_recv()

                @pl.when((p > k) & (p + 1 < n_row))
                def _():
                    row_copy(k, c, True).start()

                if k > 1:
                    @pl.when((p < k) & (p > 0))
                    def _():
                        row_copy(k, c, False).start()

    def ring_pair(s, _):
        ring_step(s, True)
        ring_step(half + s, False)
        return 0

    lax.fori_loop(0, half // 2, ring_pair, 0)
    row_step(0)

    @pl.when(pos == 0)
    def _():
        colbuf[core, rows] = rowbuf[1 - core, 0]
        lax.fori_loop(half // 2, half - 2, ring_pair, 0)

    @pl.when(pos != 0)
    def _():
        lax.fori_loop(half // 2, half - 2, ring_pair, 0)

    row_step(1)

    @pl.when(pos == 0)
    def _():
        ring(rows, after).start()
        sib(rows, core).start()

    lax.fori_loop(half - 2, half, ring_pair, 0)
    row_step(2)
    ring_step(rows, True)

    def sib_wait(block, _):
        sib(block, 1 - core).wait_recv()
        return 0

    lax.fori_loop(0, rows + 1, sib_wait, 0)
    for k in range(2):
        @pl.when(p != k)
        def _(k=k):
            for kind in range(2):
                to(small.at[k, kind], small.at[k, kind], sm_send.at[kind, 0], sm_recv.at[k, kind], p, sibling).wait_recv()
    row_step(3)

    p0h, p0l = split(piv[0])
    p1h, p1l = split(piv[1])
    u01h, u01l = split(colbuf[1, rows])
    c10h, c10l = split(colbuf[0, rows])
    l10 = mul(c10h, p0h, NN) + mul(c10h, p0l, NN) + mul(c10l, p0h, NN)
    l10h, l10l = split(l10)
    y0 = stack(small[0, 0])
    y1 = stack(small[1, 0] - thin(y0, l10h, l10l, NT))
    wloc[...] = jnp.zeros_like(wloc)

    def form(a, _):
        index = a * n_row + p
        raw0, raw1 = colbuf[0, a], colbuf[1, a]
        l0 = jnp.where(index > 0, 1.0, 0.0) * dot3_split(raw0, p0h, p0l)
        l0h, l0l = split(l0)
        mid = raw1 - (mul(l0h, u01h, NN) + mul(l0h, u01l, NN) + mul(l0l, u01h, NN))
        below = jnp.where(index > 1, 1.0, 0.0)
        l1 = below * dot3_split(mid, p1h, p1l)
        l1h, l1l = split(l1)
        fcol[0, a] = jnp.where(index > 0, l0, raw0)
        fcol[1, a] = jnp.where(index > 1, l1, mid)
        y_out[a] = direct_rhs[a] - thin(y0, l0h, l0l, NT) - thin(y1, l1h, l1l, NT)
        za = stack(adjoint_rhs[a])
        wloc[0] += below * thin(za, l0h, l0l, NN)
        wloc[1] += below * thin(za, l1h, l1l, NN)
        return 0

    quarter = rows // 4
    for g in range(4):
        lax.fori_loop(g * quarter, (g + 1) * quarter, form, 0)
        if g < 3:
            row_step(4 + g)

    owner = q % n_row
    step = n_col // n_row
    for c in range(cols):
        @pl.when(p == owner)
        def _(c=c):
            ysel[c] = y_out[c * step + q // n_row]

    def w_copy(d):
        return to(wloc, wrecv.at[p], w_send.at[d], w_recv.at[p], (p + d) % n_row, q)

    def y_copy(d):
        return to(ysel, ysel, y_send.at[d], y_recv, (p + d) % n_row, q)

    for d in range(1, n_row):
        w_copy(d).start()

    @pl.when(p == owner)
    def _():
        for d in range(1, n_row):
            y_copy(d).start()

    for c in range(7, cols):
        row_step(c)

    def form_upper(c, _):
        u0 = rowbuf[0, c]
        u0h, u0l = split(u0)
        upper[0, c] = u0
        upper[1, c] = rowbuf[1, c] - (mul(l10h, u0h, NN) + mul(l10h, u0l, NN) + mul(l10l, u0h, NN))
        return 0

    lax.fori_loop(0, cols, form_upper, 0)

    w0, w1 = wloc[0], wloc[1]
    for d in range(1, n_row):
        peer = (p + d) % n_row
        to(wloc, wrecv.at[peer], w_send.at[d], w_recv.at[peer], peer, q).wait_recv()
        w0 = w0 + wrecv[peer, 0]
        w1 = w1 + wrecv[peer, 1]
    z1 = small[1, 1] - w1
    z1l = thin(stack(z1), l10h, l10l, NN)
    z0 = small[0, 1] - w0 - z1l
    z_out[...] = adjoint_rhs[...]
    z_out[0] = jnp.where(p == 0, z0, jnp.where(p == 1, z1, adjoint_rhs[0]))

    @pl.when(p != owner)
    def _():
        to(ysel, ysel, y_send.at[0], y_recv, p, sibling).wait_recv()

    m_load.wait()

    wz0 = stack(wloc[0] + jnp.where(p == 1, 1.0, 0.0) * z1l)
    wz1 = stack(wloc[1])
    v0 = jnp.zeros((modes, width), F32)
    v1 = jnp.zeros((modes, width), F32)
    for c in range(cols):
        inner = jnp.where(q > 1, 1.0, 0.0) if c == 0 else 1.0
        yc = stack(ysel[c])
        ypair[c] = yc
        u0h, u0l = split(upper[0, c] * inner)
        u1h, u1l = split(upper[1, c] * inner)
        v0 = v0 + thin(yc, u0h, u0l, NT)
        v1 = v1 + thin(yc, u1h, u1l, NT)
        back_p[c] = -(thin(wz0, u0h, u0l, NN) + thin(wz1, u1h, u1l, NN))
    v0 = stack(v0)
    v1 = stack(v1)

    def products(a, _):
        index = a * n_row + p
        za = stack(z_out[a])
        l0h, l0l = split(fcol[0, a] * jnp.where(index > 0, 1.0, 0.0))
        l1h, l1l = split(fcol[1, a] * jnp.where(index > 1, 1.0, 0.0))
        acc = -(thin(v0, l0h, l0l, NT) + thin(v1, l1h, l1l, NT))
        for c in range(cols):
            m = mbuf[a, c] * fill[a, c].astype(F32)
            if c == 0:
                m = jnp.where(q == 0, fcol[0, a], jnp.where(q == 1, fcol[1, a], m))
            mh, ml = split(m)
            acc = acc + thin(ypair[c], mh, ml, NT)
            back_p[c] += thin(za, mh, ml, NN)
        img_p[a] = acc
        return 0

    lax.fori_loop(0, rows, products, 0)
    for m in range(modes):
        img_t[m] = img_p[:, m, :] * scale
        back_t[m] = back_p[:, m, :] * scale

    def img_copy(d):
        dest = (q + d) % n_col
        return to(img_t.at[pl.ds(dest * img_modes, img_modes)], img_r.at[q], is_send.at[d], is_recv.at[q], p, dest)

    def back_copy(d):
        dest = (p + d) % n_row
        return to(back_t.at[pl.ds(dest * back_modes, back_modes)], back_r.at[p], bs_send.at[d], bs_recv.at[p], dest, q)

    for d in range(1, n_col):
        img_copy(d).start()
    for d in range(1, n_row):
        back_copy(d).start()

    total = img_t[pl.ds(q * img_modes, img_modes)]
    for d in range(1, n_col):
        peer = (q + d) % n_col
        to(img_r.at[peer], img_r.at[peer], is_send.at[d], is_recv.at[peer], p, peer).wait_recv()
        total = total + img_r[peer]
    image[...] = total
    total = back_t[pl.ds(p * back_modes, back_modes)]
    for d in range(1, n_row):
        peer = (p + d) % n_row
        to(back_r.at[peer], back_r.at[peer], bs_send.at[d], bs_recv.at[peer], peer, q).wait_recv()
        total = total + back_r[peer]
    back[...] = total

    for d in range(1, n_col):
        img_copy(d).wait_send()
    for d in range(1, n_row):
        back_copy(d).wait_send()
        w_copy(d).wait_send()

    @pl.when(p == owner)
    def _():
        for d in range(1, n_row):
            y_copy(d).wait_send()

    @pl.when(p < 2)
    def _():
        for d in range(1, n_row):
            for kind in range(2):
                small_copy(kind, d).wait_send()

    def drain_sib(block, _):
        sib(block, core).wait_send()
        return 0

    lax.fori_loop(0, rows + 1, drain_sib, 0)

    def drain(low, high, stop):
        @pl.when(pos != stop)
        def _():
            def one(block, _):
                ring(block, after).wait_send()
                return 0

            lax.fori_loop(low, high, one, 0)

    drain(0, half, chips - 1)
    drain(half, rows, 1)
    drain(rows, rows + 1, chips - 1)
    for k in range(2):
        @pl.when((p >= k) & (p + 1 < n_row))
        def _(k=k):
            def one(c, _):
                row_copy(k, c, True).wait_send()
                return 0

            lax.fori_loop(0, cols, one, 0)

    @pl.when(p == 1)
    def _():
        def one(c, _):
            row_copy(1, c, False).wait_send()
            return 0

        lax.fori_loop(0, cols, one, 0)


def dot3_split(a, bh, bl):
    ah, al = split(a)
    return mul(ah, bh, NN) + mul(ah, bl, NN) + mul(al, bh, NN)


def update_kernel(
    n_row, tile, fill, fcol, upper, y_in, z_in, img_in, back_in, trace,
    out, y_out, z_out, image, back, uh, ul,
):
    step = pl.program_id(0)
    p = lax.axis_index("row")
    q = lax.axis_index("col")
    cols, width = trace.shape[1], trace.shape[2]

    @pl.when(step == 0)
    def _():
        for k in range(2):
            for c in range(cols):
                high, low = split(upper[k, c])
                uh[k * width:(k + 1) * width, c * width:(c + 1) * width] = high
                ul[k * width:(k + 1) * width, c * width:(c + 1) * width] = low
        y_out[...] = y_in[...]
        z_out[...] = z_in[...]
        for m in range(img_in.shape[0]):
            image[:, m, :] = img_in[m]
        for m in range(back_in.shape[0]):
            back[:, m, :] = back_in[m]

    for t in range(tile):
        a = step * tile + t
        index = a * n_row + p
        l0h, l0l = split(fcol[0, t] * jnp.where(index > 0, 1.0, 0.0))
        l1h, l1l = split(fcol[1, t] * jnp.where(index > 1, 1.0, 0.0))
        lh = jnp.concatenate([l0h, l1h], axis=1)
        ll = jnp.concatenate([l0l, l1l], axis=1)
        for c in range(0, cols, 2):
            bh = uh[:, c * width:(c + 2) * width]
            bl = ul[:, c * width:(c + 2) * width]
            change = mul(lh, bh, NN) + mul(lh, bl, NN) + mul(ll, bh, NN)
            for e in range(2):
                value = trace[t, c + e] * fill[a, c + e].astype(F32) - change[:, e * width:(e + 1) * width]
                if c + e == 0:
                    value = jnp.where(q == 0, fcol[0, t], jnp.where(q == 1, fcol[1, t], value))
                out[t, c + e] = value


def shards(trace, fill, pivots, direct_rhs, adjoint_rhs):
    n_row, n_col = lax.axis_size("row"), lax.axis_size("col")
    rows, cols, width = trace.shape[0], trace.shape[2], trace.shape[4]
    modes = direct_rhs.shape[2]
    blocks = trace.reshape(rows, cols, width, width)
    flags = fill.reshape(rows, cols)
    direct_rhs, adjoint_rhs = direct_rhs[:, 0], adjoint_rhs[:, 0]
    mi, mb = modes // n_col, modes // n_row
    vmem = pl.BlockSpec(memory_space=pltpu.VMEM)
    smem = pl.BlockSpec(memory_space=pltpu.SMEM)
    shape = jax.ShapeDtypeStruct
    dma = pltpu.SemaphoreType.DMA
    fcol, upper, y, z, image, back = pl.pallas_call(
        functools.partial(comm_kernel, n_row, n_col),
        out_shape=(
            shape((2, rows, width, width), F32),
            shape((2, cols, width, width), F32),
            shape((rows, modes, width), F32),
            shape((rows, modes, width), F32),
            shape((mi, rows, width), F32),
            shape((mb, cols, width), F32),
        ),
        in_specs=[smem, vmem, vmem, vmem, pl.BlockSpec(memory_space=pl.ANY)],
        out_specs=[vmem] * 6,
        scratch_shapes=[
            pltpu.VMEM((2, rows + 1, width, width), F32),
            pltpu.VMEM((2, cols, width, width), F32),
            pltpu.VMEM((rows, cols, width, width), F32),
            pltpu.VMEM((2, 2, modes, width), F32),
            pltpu.VMEM((2, modes, width), F32),
            pltpu.VMEM((n_row, 2, modes, width), F32),
            pltpu.VMEM((cols, modes, width), F32),
            pltpu.VMEM((cols, 2 * modes, width), BF16),
            pltpu.VMEM((8, width), F32),
            pltpu.VMEM((rows, modes, width), F32),
            pltpu.VMEM((modes, rows, width), F32),
            pltpu.VMEM((n_col, mi, rows, width), F32),
            pltpu.VMEM((cols, modes, width), F32),
            pltpu.VMEM((modes, cols, width), F32),
            pltpu.VMEM((n_row, mb, cols, width), F32),
            dma((2,)), dma,
            dma((2, n_row)), dma((2, 2)),
            dma((rows + 1,)), dma((rows + 1,)), dma((rows + 1,)), dma((rows + 1,)),
            dma((2, cols)), dma((2, cols)), dma((2, cols)),
            dma((n_row,)), dma((n_row,)), dma((n_row,)), dma,
            dma((n_col,)), dma((n_col,)), dma((n_row,)), dma((n_row,)),
        ],
        compiler_params=pltpu.CompilerParams(
            collective_id=0, has_side_effects=True, vmem_limit_bytes=40 * 1024 * 1024
        ),
    )(flags, pivots, direct_rhs, adjoint_rhs, blocks)

    tile = 2
    whole = lambda x: pl.BlockSpec(x.shape, lambda i: (0,) * x.ndim)
    outs = (
        shape(blocks.shape, F32),
        shape(y.shape, F32),
        shape(z.shape, F32),
        shape((rows, mi, width), F32),
        shape((cols, mb, width), F32),
    )
    factored, direct, adjoint, image, back = pl.pallas_call(
        functools.partial(update_kernel, n_row, tile),
        out_shape=outs,
        grid=(rows // tile,),
        in_specs=[
            smem,
            pl.BlockSpec((2, tile, width, width), lambda i: (0, i, 0, 0)),
            whole(upper), whole(y), whole(z), whole(image), whole(back),
            pl.BlockSpec((tile, cols, width, width), lambda i: (i, 0, 0, 0)),
        ],
        out_specs=[pl.BlockSpec((tile, cols, width, width), lambda i: (i, 0, 0, 0))]
        + [whole(x) for x in outs[1:]],
        scratch_shapes=[
            pltpu.VMEM((2 * width, cols * width), BF16),
            pltpu.VMEM((2 * width, cols * width), BF16),
        ],
        compiler_params=pltpu.CompilerParams(vmem_limit_bytes=24 * 1024 * 1024),
    )(flags, fcol, upper, y, z, image, back, blocks)
    return (
        factored[:, None, :, None],
        direct[:, None],
        adjoint[:, None],
        image[:, None],
        back[:, None],
    )


def solution(mesh):
    placed = (
        P(None, "row", None, "col", None, None),
        P(None, "row", None, "col"),
        P(),
        P(None, "row", None, None),
        P(None, "row", None, None),
    )
    return jax.shard_map(
        shards,
        mesh=mesh,
        in_specs=placed,
        out_specs=(
            P(None, "row", None, "col", None, None),
            P(None, "row", None, None),
            P(None, "row", None, None),
            P(None, "row", "col", None),
            P(None, "col", "row", None),
        ),
        check_vma=False,
    )
```

```python
import functools

import jax
import jax.numpy as jnp
from jax import lax
from jax.experimental import pallas as pl
from jax.experimental.pallas import tpu as pltpu
from jax.sharding import PartitionSpec as P

F32 = jnp.float32
BF16 = jnp.bfloat16
NN = (((1,), (0,)), ((), ()))
NT = (((1,), (1,)), ((), ()))


def split(x):
    high = x.astype(BF16)
    return high, (x - high.astype(F32)).astype(BF16)


def mul(a, b, dims):
    return lax.dot_general(a, b, dims, preferred_element_type=F32)


def dot3(a, b, dims):
    ah, al = split(a)
    bh, bl = split(b)
    return mul(ah, bh, dims) + mul(ah, bl, dims) + mul(al, bh, dims)


def stack(x):
    high, low = split(x)
    return jnp.concatenate([high, low], axis=0)


def thin(pair, bh, bl, dims):
    half = pair.shape[0] // 2
    both = mul(pair, bh, dims)
    return both[:half] + both[half:] + mul(pair[:half], bl, dims)


def comm_kernel(
    n_row, n_col, fill, piv, direct_rhs, adjoint_rhs, trace,
    fcol, upper, y_out, z_out, image, back,
    colbuf, rowbuf, small, wloc, wrecv, ysel, ypair, zpair,
    img_p, img_t, img_r, back_p, back_t, back_r,
    sm_send, sm_recv, ring_send, ring_recv, sib_send, sib_recv,
    row_up, row_down, row_recv, w_send, w_recv, y_send, y_recv,
    is_send, is_recv, bs_send, bs_recv,
):
    rows, cols = trace.shape[0], trace.shape[1]
    modes = y_out.shape[1]
    width = y_out.shape[2]
    img_modes, back_modes = modes // n_col, modes // n_row
    scale = (rows * n_row * width) ** (-0.5)
    p = lax.axis_index("row")
    q = lax.axis_index("col")
    chips = n_col // 2
    deep = chips // 2
    chip, core = q // 2, q % 2
    cy, cx = chip // 2, chip % 2
    pos = cx * (cy + 1) + (1 - cx) * ((chips - cy) % chips)

    def at_pos(r):
        side = 1 - ((r + chips - 1) % chips) // deep
        return (side * ((r - 1) * 2 + 1) + (1 - side) * (((chips - r) % chips) * 2)) * 2 + core

    after = at_pos((pos + 1) % chips)
    before = at_pos((pos + chips - 1) % chips)
    sibling = chip * 2 + 1 - core
    half = rows // 2

    def to(src, dst, send, recv, row, col):
        return pltpu.make_async_remote_copy(
            src_ref=src, dst_ref=dst, send_sem=send, recv_sem=recv,
            device_id=(row, col), device_id_type=pl.DeviceIdType.MESH,
        )

    barrier = pltpu.get_barrier_semaphore()
    for d in range(1, n_col):
        pl.semaphore_signal(barrier, inc=1, device_id=(p, (q + d) % n_col), device_id_type=pl.DeviceIdType.MESH)
    for d in range(1, n_row):
        pl.semaphore_signal(barrier, inc=1, device_id=((p + d) % n_row, q), device_id_type=pl.DeviceIdType.MESH)

    @pl.when(q < 2)
    def _():
        def mask(a, _):
            colbuf[core, a] = trace[a, 0] * fill[a, 0].astype(F32)
            return 0

        lax.fori_loop(0, rows, mask, 0)

    @pl.when(p < 2)
    def _():
        slot = lax.rem(p, 2)

        def mask(c, _):
            rowbuf[slot, c] = trace[0, c] * fill[0, c].astype(F32)
            return 0

        lax.fori_loop(0, cols, mask, 0)
        small[slot, 0] = direct_rhs[0]
        small[slot, 1] = adjoint_rhs[0]

    pl.semaphore_wait(barrier, n_col + n_row - 2)

    def small_copy(kind, d):
        src = (direct_rhs, adjoint_rhs)[kind].at[0]
        return to(src, small.at[lax.rem(p, 2), kind], sm_send.at[kind, d], sm_recv.at[lax.rem(p, 2), kind], (p + d) % n_row, q)

    def ring(block, dest):
        ref = colbuf.at[core, block]
        return to(ref, ref, ring_send.at[block], ring_recv.at[block], p, dest)

    def sib(block, which):
        ref = colbuf.at[which, block]
        return to(ref, ref, sib_send.at[block], sib_recv.at[block], p, sibling)

    def row_copy(k, c, upward):
        ref = rowbuf.at[k, c]
        sems = row_up if upward else row_down
        dest = lax.rem(p + (1 if upward else n_row - 1), n_row)
        return to(ref, ref, sems.at[k, c], row_recv.at[k, c], dest, q)

    @pl.when(pos == 0)
    def _():
        def send(s, _):
            ring(s, after).start()
            ring(half + s, before).start()
            return 0

        lax.fori_loop(0, half, send, 0)

    for k in range(2):
        @pl.when(p == k)
        def _(k=k):
            def send(c, _):
                if k + 1 < n_row:
                    row_copy(k, c, True).start()
                if k > 0:
                    row_copy(k, c, False).start()
                return 0

            lax.fori_loop(0, cols, send, 0)

    @pl.when(p < 2)
    def _():
        for d in range(1, n_row):
            for kind in range(2):
                small_copy(kind, d).start()

    @pl.when(pos == 0)
    def _():
        def send(s, _):
            sib(s, core).start()
            return 0

        lax.fori_loop(0, rows, send, 0)

    def ring_step(block, forward):
        @pl.when(pos != 0)
        def _():
            dest = after if forward else before
            ring(block, dest).wait_recv()
            stop = chips - 1 if forward else 1

            @pl.when(pos != stop)
            def _():
                ring(block, dest).start()

            sib(block, core).start()

    def row_step(c):
        for k in range(2):
            @pl.when(p != k)
            def _(k=k):
                row_copy(k, c, True).wait_recv()

                @pl.when((p > k) & (p + 1 < n_row))
                def _():
                    row_copy(k, c, True).start()

                if k > 1:
                    @pl.when((p < k) & (p > 0))
                    def _():
                        row_copy(k, c, False).start()

    def corner(dest, send, recv):
        return to(rowbuf.at[1 - core, 0], colbuf.at[core, rows], send.at[rows], recv.at[rows], p, dest)

    def back_row(a, first):
        za = stack(adjoint_rhs[a])
        for c in range(first, cols):
            mh, ml = split(trace[a, c] * fill[a, c].astype(F32))
            back_p[c] += thin(za, mh, ml, NN)

    back_p[...] = jnp.zeros_like(back_p)
    lag = 2
    row_lag = 3
    base = row_lag * jnp.maximum(p, 1)
    ticks = max(half + lag * (chips - 1), row_lag * max(n_row - 1, 1) + lag * (chips - 1) + 2, rows)
    last = n_row - 1

    def row_tick(k):
        d = k - base

        @pl.when((d >= 0) & (d < 2 * cols) & ((d == 0) | (p != last)))
        def _():
            @pl.when(lax.rem(d, 2) == 0)
            def _():
                row_step(lax.div(d, 2))

    def tick(k, _):
        sa = k - lag * pos

        @pl.when((sa >= 0) & (sa < half))
        def _():
            ring_step(sa, True)

        sb = k - lag * (chips - pos)

        @pl.when((sb >= 0) & (sb < half))
        def _():
            ring_step(half + sb, False)

        row_tick(k)

        @pl.when((pos == 0) & (k == base))
        def _():
            corner(after, ring_send, ring_recv).start()
            corner(sibling, sib_send, sib_recv).start()
            colbuf[core, rows] = rowbuf[1 - core, 0]

        @pl.when(k == base + lag * pos + 1)
        def _():
            ring_step(rows, True)

        @pl.when((k >= 1) & (k < rows))
        def _():
            back_row(k, 1)

        return 0

    lax.fori_loop(0, ticks, tick, 0)

    def sib_wait(block, _):
        sib(block, 1 - core).wait_recv()
        return 0

    lax.fori_loop(0, rows + 1, sib_wait, 0)
    for k in range(2):
        @pl.when(p != k)
        def _(k=k):
            for kind in range(2):
                to(small.at[k, kind], small.at[k, kind], sm_send.at[kind, 0], sm_recv.at[k, kind], p, sibling).wait_recv()

    p0h, p0l = split(piv[0])
    p1h, p1l = split(piv[1])
    u01h, u01l = split(colbuf[1, rows])
    c10h, c10l = split(colbuf[0, rows])
    l10 = mul(c10h, p0h, NN) + mul(c10h, p0l, NN) + mul(c10l, p0h, NN)
    l10h, l10l = split(l10)
    y0 = stack(small[0, 0])
    y1 = stack(small[1, 0] - thin(y0, l10h, l10l, NT))
    wloc[...] = jnp.zeros_like(wloc)

    def form(a, _):
        index = a * n_row + p
        raw0, raw1 = colbuf[0, a], colbuf[1, a]
        l0 = jnp.where(index > 0, 1.0, 0.0) * dot3_split(raw0, p0h, p0l)
        l0h, l0l = split(l0)
        mid = raw1 - (mul(l0h, u01h, NN) + mul(l0h, u01l, NN) + mul(l0l, u01h, NN))
        below = jnp.where(index > 1, 1.0, 0.0)
        l1 = below * dot3_split(mid, p1h, p1l)
        l1h, l1l = split(l1)
        fcol[0, a] = jnp.where(index > 0, l0, raw0)
        fcol[1, a] = jnp.where(index > 1, l1, mid)
        y_out[a] = direct_rhs[a] - thin(y0, l0h, l0l, NT) - thin(y1, l1h, l1l, NT)
        za = stack(adjoint_rhs[a])
        wloc[0] += below * thin(za, l0h, l0l, NN)
        wloc[1] += below * thin(za, l1h, l1l, NN)
        return 0

    quarter = rows // 4
    for g in range(4):
        lax.fori_loop(g * quarter, (g + 1) * quarter, form, 0)
        row_tick(ticks + 2 * g)
        row_tick(ticks + 2 * g + 1)

    owner = q % n_row
    step = n_col // n_row
    for c in range(cols):
        @pl.when(p == owner)
        def _(c=c):
            ysel[c] = y_out[c * step + q // n_row]

    def w_copy(d):
        return to(wloc, wrecv.at[p], w_send.at[d], w_recv.at[p], (p + d) % n_row, q)

    def y_copy(d):
        return to(ysel, ysel, y_send.at[d], y_recv, (p + d) % n_row, q)

    for d in range(1, n_row):
        w_copy(d).start()

    @pl.when(p == owner)
    def _():
        for d in range(1, n_row):
            y_copy(d).start()

    def late(k, _):
        row_tick(k)
        return 0

    lax.fori_loop(ticks + 8, max(ticks + 8, row_lag * max(n_row - 1, 1) + 2 * cols), late, 0)

    @pl.when(p == last)
    def _():
        def arrive(c, _):
            row_step(c)
            return 0

        lax.fori_loop(1, cols, arrive, 0)

    def form_upper(c, _):
        u0 = rowbuf[0, c]
        u0h, u0l = split(u0)
        upper[0, c] = u0
        upper[1, c] = rowbuf[1, c] - (mul(l10h, u0h, NN) + mul(l10h, u0l, NN) + mul(l10l, u0h, NN))
        return 0

    lax.fori_loop(0, cols, form_upper, 0)

    w0, w1 = wloc[0], wloc[1]
    for d in range(1, n_row):
        peer = (p + d) % n_row
        to(wloc, wrecv.at[peer], w_send.at[d], w_recv.at[peer], peer, q).wait_recv()
        w0 = w0 + wrecv[peer, 0]
        w1 = w1 + wrecv[peer, 1]
    z1 = small[1, 1] - w1
    z1l = thin(stack(z1), l10h, l10l, NN)
    z0 = small[0, 1] - w0 - z1l
    z_out[...] = adjoint_rhs[...]
    z_out[0] = jnp.where(p == 0, z0, jnp.where(p == 1, z1, adjoint_rhs[0]))

    @pl.when(p != owner)
    def _():
        to(ysel, ysel, y_send.at[0], y_recv, p, sibling).wait_recv()

    wz0 = stack(wloc[0] + jnp.where(p == 1, 1.0, 0.0) * z1l)
    wz1 = stack(wloc[1])
    v0 = jnp.zeros((modes, width), F32)
    v1 = jnp.zeros((modes, width), F32)
    for c in range(cols):
        inner = jnp.where(q > 1, 1.0, 0.0) if c == 0 else 1.0
        yc = stack(ysel[c])
        ypair[c] = yc
        u0h, u0l = split(upper[0, c] * inner)
        u1h, u1l = split(upper[1, c] * inner)
        v0 = v0 + thin(yc, u0h, u0l, NT)
        v1 = v1 + thin(yc, u1h, u1l, NT)
        back_p[c] -= (thin(wz0, u0h, u0l, NN) + thin(wz1, u1h, u1l, NN))
    v0 = stack(v0)
    v1 = stack(v1)

    def products(a, _):
        index = a * n_row + p
        za = stack(z_out[a])
        l0h, l0l = split(fcol[0, a] * jnp.where(index > 0, 1.0, 0.0))
        l1h, l1l = split(fcol[1, a] * jnp.where(index > 1, 1.0, 0.0))
        acc = -(thin(v0, l0h, l0l, NT) + thin(v1, l1h, l1l, NT))
        for c in range(cols):
            m = trace[a, c] * fill[a, c].astype(F32)
            if c == 0:
                m = jnp.where(q == 0, fcol[0, a], jnp.where(q == 1, fcol[1, a], m))
            mh, ml = split(m)
            acc = acc + thin(ypair[c], mh, ml, NT)
            if c == 0:
                back_p[c] += thin(za, mh, ml, NN)
        img_p[a] = acc
        return 0

    lax.fori_loop(0, rows, products, 0)
    first = stack(z_out[0])
    for c in range(1, cols):
        mh, ml = split(trace[0, c] * fill[0, c].astype(F32))
        back_p[c] += thin(first, mh, ml, NN)
    for m in range(modes):
        img_t[m] = img_p[:, m, :] * scale
        back_t[m] = back_p[:, m, :] * scale

    def img_copy(d):
        dest = (q + d) % n_col
        return to(img_t.at[pl.ds(dest * img_modes, img_modes)], img_r.at[q], is_send.at[d], is_recv.at[q], p, dest)

    def back_copy(d):
        dest = (p + d) % n_row
        return to(back_t.at[pl.ds(dest * back_modes, back_modes)], back_r.at[p], bs_send.at[d], bs_recv.at[p], dest, q)

    for d in range(1, n_col):
        img_copy(d).start()
    for d in range(1, n_row):
        back_copy(d).start()

    total = img_t[pl.ds(q * img_modes, img_modes)]
    for d in range(1, n_col):
        peer = (q + d) % n_col
        to(img_r.at[peer], img_r.at[peer], is_send.at[d], is_recv.at[peer], p, peer).wait_recv()
        total = total + img_r[peer]
    image[...] = total
    total = back_t[pl.ds(p * back_modes, back_modes)]
    for d in range(1, n_row):
        peer = (p + d) % n_row
        to(back_r.at[peer], back_r.at[peer], bs_send.at[d], bs_recv.at[peer], peer, q).wait_recv()
        total = total + back_r[peer]
    back[...] = total

    for d in range(1, n_col):
        img_copy(d).wait_send()
    for d in range(1, n_row):
        back_copy(d).wait_send()
        w_copy(d).wait_send()

    @pl.when(p == owner)
    def _():
        for d in range(1, n_row):
            y_copy(d).wait_send()

    @pl.when(p < 2)
    def _():
        for d in range(1, n_row):
            for kind in range(2):
                small_copy(kind, d).wait_send()

    def drain_sib(block, _):
        sib(block, core).wait_send()
        return 0

    lax.fori_loop(0, rows + 1, drain_sib, 0)

    def drain(low, high, stop):
        @pl.when(pos != stop)
        def _():
            def one(block, _):
                ring(block, after).wait_send()
                return 0

            lax.fori_loop(low, high, one, 0)

    drain(0, half, chips - 1)
    drain(half, rows, 1)
    drain(rows, rows + 1, chips - 1)
    for k in range(2):
        @pl.when((p >= k) & (p + 1 < n_row))
        def _(k=k):
            def one(c, _):
                row_copy(k, c, True).wait_send()
                return 0

            lax.fori_loop(0, cols, one, 0)

    @pl.when(p == 1)
    def _():
        def one(c, _):
            row_copy(1, c, False).wait_send()
            return 0

        lax.fori_loop(0, cols, one, 0)


def dot3_split(a, bh, bl):
    ah, al = split(a)
    return mul(ah, bh, NN) + mul(ah, bl, NN) + mul(al, bh, NN)


def update_kernel(
    n_row, tile, fill, fcol, upper, y_in, z_in, img_in, back_in, trace,
    out, y_out, z_out, image, back, uh, ul,
):
    step = pl.program_id(0)
    p = lax.axis_index("row")
    q = lax.axis_index("col")
    cols, width = trace.shape[1], trace.shape[2]

    @pl.when(step == 0)
    def _():
        for k in range(2):
            for c in range(cols):
                high, low = split(upper[k, c])
                uh[k * width:(k + 1) * width, c * width:(c + 1) * width] = high
                ul[k * width:(k + 1) * width, c * width:(c + 1) * width] = low
        y_out[...] = y_in[...]
        z_out[...] = z_in[...]
        for m in range(img_in.shape[0]):
            image[:, m, :] = img_in[m]
        for m in range(back_in.shape[0]):
            back[:, m, :] = back_in[m]

    for t in range(tile):
        a = step * tile + t
        index = a * n_row + p
        l0h, l0l = split(fcol[0, t] * jnp.where(index > 0, 1.0, 0.0))
        l1h, l1l = split(fcol[1, t] * jnp.where(index > 1, 1.0, 0.0))
        lh = jnp.concatenate([l0h, l1h], axis=1)
        ll = jnp.concatenate([l0l, l1l], axis=1)
        for c in range(0, cols, 2):
            bh = uh[:, c * width:(c + 2) * width]
            bl = ul[:, c * width:(c + 2) * width]
            change = mul(lh, bh, NN) + mul(lh, bl, NN) + mul(ll, bh, NN)
            for e in range(2):
                value = trace[t, c + e] * fill[a, c + e].astype(F32) - change[:, e * width:(e + 1) * width]
                if c + e == 0:
                    value = jnp.where(q == 0, fcol[0, t], jnp.where(q == 1, fcol[1, t], value))
                out[t, c + e] = value


def shards(trace, fill, pivots, direct_rhs, adjoint_rhs):
    n_row, n_col = lax.axis_size("row"), lax.axis_size("col")
    rows, cols, width = trace.shape[0], trace.shape[2], trace.shape[4]
    modes = direct_rhs.shape[2]
    blocks = trace.reshape(rows, cols, width, width)
    flags = fill.reshape(rows, cols)
    direct_rhs, adjoint_rhs = direct_rhs[:, 0], adjoint_rhs[:, 0]
    mi, mb = modes // n_col, modes // n_row
    vmem = pl.BlockSpec(memory_space=pltpu.VMEM)
    smem = pl.BlockSpec(memory_space=pltpu.SMEM)
    shape = jax.ShapeDtypeStruct
    dma = pltpu.SemaphoreType.DMA
    fcol, upper, y, z, image, back = pl.pallas_call(
        functools.partial(comm_kernel, n_row, n_col),
        out_shape=(
            shape((2, rows, width, width), F32),
            shape((2, cols, width, width), F32),
            shape((rows, modes, width), F32),
            shape((rows, modes, width), F32),
            shape((mi, rows, width), F32),
            shape((mb, cols, width), F32),
        ),
        in_specs=[smem, vmem, vmem, vmem, vmem],
        out_specs=[vmem] * 6,
        scratch_shapes=[
            pltpu.VMEM((2, rows + 1, width, width), F32),
            pltpu.VMEM((2, cols, width, width), F32),
            pltpu.VMEM((2, 2, modes, width), F32),
            pltpu.VMEM((2, modes, width), F32),
            pltpu.VMEM((n_row, 2, modes, width), F32),
            pltpu.VMEM((cols, modes, width), F32),
            pltpu.VMEM((cols, 2 * modes, width), BF16),
            pltpu.VMEM((8, width), F32),
            pltpu.VMEM((rows, modes, width), F32),
            pltpu.VMEM((modes, rows, width), F32),
            pltpu.VMEM((n_col, mi, rows, width), F32),
            pltpu.VMEM((cols, modes, width), F32),
            pltpu.VMEM((modes, cols, width), F32),
            pltpu.VMEM((n_row, mb, cols, width), F32),
            dma((2, n_row)), dma((2, 2)),
            dma((rows + 1,)), dma((rows + 1,)), dma((rows + 1,)), dma((rows + 1,)),
            dma((2, cols)), dma((2, cols)), dma((2, cols)),
            dma((n_row,)), dma((n_row,)), dma((n_row,)), dma,
            dma((n_col,)), dma((n_col,)), dma((n_row,)), dma((n_row,)),
        ],
        compiler_params=pltpu.CompilerParams(
            collective_id=0, has_side_effects=True, vmem_limit_bytes=40 * 1024 * 1024
        ),
    )(flags, pivots, direct_rhs, adjoint_rhs, blocks)

    tile = 2
    whole = lambda x: pl.BlockSpec(x.shape, lambda i: (0,) * x.ndim)
    outs = (
        shape(blocks.shape, F32),
        shape(y.shape, F32),
        shape(z.shape, F32),
        shape((rows, mi, width), F32),
        shape((cols, mb, width), F32),
    )
    factored, direct, adjoint, image, back = pl.pallas_call(
        functools.partial(update_kernel, n_row, tile),
        out_shape=outs,
        grid=(rows // tile,),
        in_specs=[
            smem,
            pl.BlockSpec((2, tile, width, width), lambda i: (0, i, 0, 0)),
            whole(upper), whole(y), whole(z), whole(image), whole(back),
            pl.BlockSpec((tile, cols, width, width), lambda i: (i, 0, 0, 0)),
        ],
        out_specs=[pl.BlockSpec((tile, cols, width, width), lambda i: (i, 0, 0, 0))]
        + [whole(x) for x in outs[1:]],
        scratch_shapes=[
            pltpu.VMEM((2 * width, cols * width), BF16),
            pltpu.VMEM((2 * width, cols * width), BF16),
        ],
        compiler_params=pltpu.CompilerParams(vmem_limit_bytes=24 * 1024 * 1024),
    )(flags, fcol, upper, y, z, image, back, blocks)
    return (
        factored[:, None, :, None],
        direct[:, None],
        adjoint[:, None],
        image[:, None],
        back[:, None],
    )


def solution(mesh):
    placed = (
        P(None, "row", None, "col", None, None),
        P(None, "row", None, "col"),
        P(),
        P(None, "row", None, None),
        P(None, "row", None, None),
    )
    return jax.shard_map(
        shards,
        mesh=mesh,
        in_specs=placed,
        out_specs=(
            P(None, "row", None, "col", None, None),
            P(None, "row", None, None),
            P(None, "row", None, None),
            P(None, "row", "col", None),
            P(None, "col", "row", None),
        ),
        check_vma=False,
    )
```

```python
import functools

import jax
import jax.numpy as jnp
from jax import lax
from jax.experimental import pallas as pl
from jax.experimental.pallas import tpu as pltpu
from jax.sharding import PartitionSpec as P

F32 = jnp.float32
BF16 = jnp.bfloat16
NN = (((1,), (0,)), ((), ()))
NT = (((1,), (1,)), ((), ()))


def split(x):
    high = x.astype(BF16)
    return high, (x - high.astype(F32)).astype(BF16)


def mul(a, b, dims):
    return lax.dot_general(a, b, dims, preferred_element_type=F32)


def dot3(a, b, dims):
    ah, al = split(a)
    bh, bl = split(b)
    return mul(ah, bh, dims) + mul(ah, bl, dims) + mul(al, bh, dims)


def stack(x):
    high, low = split(x)
    return jnp.concatenate([high, low], axis=0)


def thin(pair, bh, bl, dims):
    half = pair.shape[0] // 2
    both = mul(pair, bh, dims)
    return both[:half] + both[half:] + mul(pair[:half], bl, dims)


def comm_kernel(
    n_row, n_col, fill, packed, trace,
    fcol, upper, y_out, z_out, image, back,
    colbuf, rowbuf, small, wloc, wrecv, ysel, ypair, zpair,
    img_p, img_t, img_r, back_p, back_t, back_r,
    sm_send, sm_recv, ring_send, ring_recv, sib_send, sib_recv,
    row_up, row_down, row_recv, w_send, w_recv, y_send, y_recv,
    is_send, is_recv, bs_send, bs_recv,
):
    rows, cols = trace.shape[0], trace.shape[1]
    direct_rhs, adjoint_rhs = packed.at[0], packed.at[1]
    modes = y_out.shape[1]
    width = y_out.shape[2]
    img_modes, back_modes = modes // n_col, modes // n_row
    scale = (rows * n_row * width) ** (-0.5)
    p = lax.axis_index("row")
    q = lax.axis_index("col")
    chips = n_col // 2
    deep = chips // 2
    chip, core = q // 2, q % 2
    cy, cx = chip // 2, chip % 2
    pos = cx * (cy + 1) + (1 - cx) * ((chips - cy) % chips)

    def at_pos(r):
        side = 1 - ((r + chips - 1) % chips) // deep
        return (side * ((r - 1) * 2 + 1) + (1 - side) * (((chips - r) % chips) * 2)) * 2 + core

    after = at_pos((pos + 1) % chips)
    before = at_pos((pos + chips - 1) % chips)
    sibling = chip * 2 + 1 - core
    half = rows // 2

    def to(src, dst, send, recv, row, col):
        return pltpu.make_async_remote_copy(
            src_ref=src, dst_ref=dst, send_sem=send, recv_sem=recv,
            device_id=(row, col), device_id_type=pl.DeviceIdType.MESH,
        )

    barrier = pltpu.get_barrier_semaphore()
    for d in range(1, n_col):
        pl.semaphore_signal(barrier, inc=1, device_id=(p, (q + d) % n_col), device_id_type=pl.DeviceIdType.MESH)
    for d in range(1, n_row):
        pl.semaphore_signal(barrier, inc=1, device_id=((p + d) % n_row, q), device_id_type=pl.DeviceIdType.MESH)

    @pl.when(q < 2)
    def _():
        def mask(a, _):
            colbuf[core, a] = trace[a, 0] * fill[a, 0].astype(F32)
            return 0

        lax.fori_loop(0, rows, mask, 0)

    @pl.when(p < 2)
    def _():
        slot = lax.rem(p, 2)

        def mask(c, _):
            rowbuf[slot, c] = trace[0, c] * fill[0, c].astype(F32)
            return 0

        lax.fori_loop(0, cols, mask, 0)
        small[slot, 0] = direct_rhs[0]
        small[slot, 1] = adjoint_rhs[0]

    pl.semaphore_wait(barrier, n_col + n_row - 2)

    def small_copy(kind, d):
        src = (direct_rhs, adjoint_rhs)[kind].at[0]
        return to(src, small.at[lax.rem(p, 2), kind], sm_send.at[kind, d], sm_recv.at[lax.rem(p, 2), kind], (p + d) % n_row, q)

    def ring(block, dest):
        ref = colbuf.at[core, block]
        return to(ref, ref, ring_send.at[block], ring_recv.at[block], p, dest)

    def sib(block, which):
        ref = colbuf.at[which, block]
        return to(ref, ref, sib_send.at[block], sib_recv.at[block], p, sibling)

    def row_copy(k, c, upward):
        ref = rowbuf.at[k, c]
        sems = row_up if upward else row_down
        dest = lax.rem(p + (1 if upward else n_row - 1), n_row)
        return to(ref, ref, sems.at[k, c], row_recv.at[k, c], dest, q)

    @pl.when(pos == 0)
    def _():
        def send(s, _):
            ring(s, after).start()
            ring(half + s, before).start()
            return 0

        lax.fori_loop(0, half, send, 0)

    for k in range(2):
        @pl.when(p == k)
        def _(k=k):
            def send(c, _):
                if k + 1 < n_row:
                    row_copy(k, c, True).start()
                if k > 0:
                    row_copy(k, c, False).start()
                return 0

            lax.fori_loop(0, cols, send, 0)

    @pl.when(p < 2)
    def _():
        for d in range(1, n_row):
            for kind in range(2):
                small_copy(kind, d).start()

    @pl.when(pos == 0)
    def _():
        def send(s, _):
            sib(s, core).start()
            return 0

        lax.fori_loop(0, rows, send, 0)

    def ring_step(block, forward):
        @pl.when(pos != 0)
        def _():
            dest = after if forward else before
            ring(block, dest).wait_recv()
            stop = chips - 1 if forward else 1

            @pl.when(pos != stop)
            def _():
                ring(block, dest).start()

            sib(block, core).start()

    def row_step(c):
        for k in range(2):
            @pl.when(p != k)
            def _(k=k):
                row_copy(k, c, True).wait_recv()

                @pl.when((p > k) & (p + 1 < n_row))
                def _():
                    row_copy(k, c, True).start()

                if k > 1:
                    @pl.when((p < k) & (p > 0))
                    def _():
                        row_copy(k, c, False).start()

    def corner(dest, send, recv):
        return to(rowbuf.at[1 - core, 0], colbuf.at[core, rows], send.at[rows], recv.at[rows], p, dest)

    def back_row(a, first):
        za = stack(adjoint_rhs[a])
        for c in range(first, cols):
            mh, ml = split(trace[a, c] * fill[a, c].astype(F32))
            back_p[c] += thin(za, mh, ml, NN)

    back_p[...] = jnp.zeros_like(back_p)
    lag = 2
    row_lag = 4
    stride = 2
    base = row_lag * jnp.maximum(p, 1)
    ticks = max(half + lag * (chips - 1), row_lag * max(n_row - 1, 1) + lag * (chips - 1) + 2, rows)
    last = n_row - 1

    def row_tick(k):
        d = k - base

        @pl.when((d >= 0) & (d < stride * cols) & ((d == 0) | (p != last)))
        def _():
            @pl.when(lax.rem(d, stride) == 0)
            def _():
                row_step(lax.div(d, stride))

    def tick(k, _):
        sa = k - lag * pos

        @pl.when((sa >= 0) & (sa < half))
        def _():
            ring_step(sa, True)

        sb = k - lag * (chips - pos)

        @pl.when((sb >= 0) & (sb < half))
        def _():
            ring_step(half + sb, False)

        row_tick(k)

        @pl.when((pos == 0) & (k == base))
        def _():
            corner(after, ring_send, ring_recv).start()
            corner(sibling, sib_send, sib_recv).start()
            colbuf[core, rows] = rowbuf[1 - core, 0]

        @pl.when(k == base + lag * pos + 1)
        def _():
            ring_step(rows, True)

        @pl.when((k >= 1) & (k < rows))
        def _():
            back_row(k, 1)

        return 0

    lax.fori_loop(0, ticks, tick, 0)

    def sib_wait(block, _):
        sib(block, 1 - core).wait_recv()
        return 0

    lax.fori_loop(0, rows + 1, sib_wait, 0)
    for k in range(2):
        @pl.when(p != k)
        def _(k=k):
            for kind in range(2):
                to(small.at[k, kind], small.at[k, kind], sm_send.at[kind, 0], sm_recv.at[k, kind], p, sibling).wait_recv()

    per = width // modes
    p0h, p0l = split(packed[2, 0:per].reshape(width, width))
    p1h, p1l = split(packed[2, per:2 * per].reshape(width, width))
    u01h, u01l = split(colbuf[1, rows])
    c10h, c10l = split(colbuf[0, rows])
    l10 = mul(c10h, p0h, NN) + mul(c10h, p0l, NN) + mul(c10l, p0h, NN)
    l10h, l10l = split(l10)
    y0 = stack(small[0, 0])
    y1 = stack(small[1, 0] - thin(y0, l10h, l10l, NT))
    wloc[...] = jnp.zeros_like(wloc)

    def form(a, _):
        index = a * n_row + p
        raw0, raw1 = colbuf[0, a], colbuf[1, a]
        l0 = jnp.where(index > 0, 1.0, 0.0) * dot3_split(raw0, p0h, p0l)
        l0h, l0l = split(l0)
        mid = raw1 - (mul(l0h, u01h, NN) + mul(l0h, u01l, NN) + mul(l0l, u01h, NN))
        below = jnp.where(index > 1, 1.0, 0.0)
        l1 = below * dot3_split(mid, p1h, p1l)
        l1h, l1l = split(l1)
        fcol[0, a] = jnp.where(index > 0, l0, raw0)
        fcol[1, a] = jnp.where(index > 1, l1, mid)
        y_out[a] = direct_rhs[a] - thin(y0, l0h, l0l, NT) - thin(y1, l1h, l1l, NT)
        za = stack(adjoint_rhs[a])
        wloc[0] += below * thin(za, l0h, l0l, NN)
        wloc[1] += below * thin(za, l1h, l1l, NN)
        return 0

    quarter = rows // 4
    for g in range(4):
        lax.fori_loop(g * quarter, (g + 1) * quarter, form, 0)
        row_tick(ticks + 2 * g)
        row_tick(ticks + 2 * g + 1)

    owner = q % n_row
    step = n_col // n_row
    for c in range(cols):
        @pl.when(p == owner)
        def _(c=c):
            ysel[c] = y_out[c * step + q // n_row]

    def w_copy(d):
        return to(wloc, wrecv.at[p], w_send.at[d], w_recv.at[p], (p + d) % n_row, q)

    def y_copy(d):
        return to(ysel, ysel, y_send.at[d], y_recv, (p + d) % n_row, q)

    for d in range(1, n_row):
        w_copy(d).start()

    @pl.when(p == owner)
    def _():
        for d in range(1, n_row):
            y_copy(d).start()

    def late(k, _):
        row_tick(k)
        return 0

    lax.fori_loop(ticks + 8, max(ticks + 8, row_lag * max(n_row - 1, 1) + stride * cols), late, 0)

    @pl.when(p == last)
    def _():
        def arrive(c, _):
            row_step(c)
            return 0

        lax.fori_loop(1, cols, arrive, 0)

    def form_upper(c, _):
        u0 = rowbuf[0, c]
        u0h, u0l = split(u0)
        upper[0, c] = u0
        upper[1, c] = rowbuf[1, c] - (mul(l10h, u0h, NN) + mul(l10h, u0l, NN) + mul(l10l, u0h, NN))
        return 0

    lax.fori_loop(0, cols, form_upper, 0)

    w0, w1 = wloc[0], wloc[1]
    for d in range(1, n_row):
        peer = (p + d) % n_row
        to(wloc, wrecv.at[peer], w_send.at[d], w_recv.at[peer], peer, q).wait_recv()
        w0 = w0 + wrecv[peer, 0]
        w1 = w1 + wrecv[peer, 1]
    z1 = small[1, 1] - w1
    z1l = thin(stack(z1), l10h, l10l, NN)
    z0 = small[0, 1] - w0 - z1l
    z_out[...] = adjoint_rhs[...]
    z_out[0] = jnp.where(p == 0, z0, jnp.where(p == 1, z1, adjoint_rhs[0]))

    @pl.when(p != owner)
    def _():
        to(ysel, ysel, y_send.at[0], y_recv, p, sibling).wait_recv()

    wz0 = stack(wloc[0] + jnp.where(p == 1, 1.0, 0.0) * z1l)
    wz1 = stack(wloc[1])
    v0 = jnp.zeros((modes, width), F32)
    v1 = jnp.zeros((modes, width), F32)
    for c in range(cols):
        inner = jnp.where(q > 1, 1.0, 0.0) if c == 0 else 1.0
        yc = stack(ysel[c])
        ypair[c] = yc
        u0h, u0l = split(upper[0, c] * inner)
        u1h, u1l = split(upper[1, c] * inner)
        v0 = v0 + thin(yc, u0h, u0l, NT)
        v1 = v1 + thin(yc, u1h, u1l, NT)
        back_p[c] -= (thin(wz0, u0h, u0l, NN) + thin(wz1, u1h, u1l, NN))
    v0 = stack(v0)
    v1 = stack(v1)

    def products(a, _):
        index = a * n_row + p
        za = stack(z_out[a])
        l0h, l0l = split(fcol[0, a] * jnp.where(index > 0, 1.0, 0.0))
        l1h, l1l = split(fcol[1, a] * jnp.where(index > 1, 1.0, 0.0))
        acc = -(thin(v0, l0h, l0l, NT) + thin(v1, l1h, l1l, NT))
        for c in range(cols):
            m = trace[a, c] * fill[a, c].astype(F32)
            if c == 0:
                m = jnp.where(q == 0, fcol[0, a], jnp.where(q == 1, fcol[1, a], m))
            mh, ml = split(m)
            acc = acc + thin(ypair[c], mh, ml, NT)
            if c == 0:
                back_p[c] += thin(za, mh, ml, NN)
        img_p[a] = acc
        return 0

    lax.fori_loop(0, rows, products, 0)
    first = stack(z_out[0])
    for c in range(1, cols):
        mh, ml = split(trace[0, c] * fill[0, c].astype(F32))
        back_p[c] += thin(first, mh, ml, NN)
    for m in range(modes):
        img_t[m] = img_p[:, m, :] * scale
        back_t[m] = back_p[:, m, :] * scale

    def img_copy(d):
        dest = (q + d) % n_col
        return to(img_t.at[pl.ds(dest * img_modes, img_modes)], img_r.at[q], is_send.at[d], is_recv.at[q], p, dest)

    def back_copy(d):
        dest = (p + d) % n_row
        return to(back_t.at[pl.ds(dest * back_modes, back_modes)], back_r.at[p], bs_send.at[d], bs_recv.at[p], dest, q)

    for d in range(1, n_col):
        img_copy(d).start()
    for d in range(1, n_row):
        back_copy(d).start()

    total = img_t[pl.ds(q * img_modes, img_modes)]
    for d in range(1, n_col):
        peer = (q + d) % n_col
        to(img_r.at[peer], img_r.at[peer], is_send.at[d], is_recv.at[peer], p, peer).wait_recv()
        total = total + img_r[peer]
    image[...] = total
    total = back_t[pl.ds(p * back_modes, back_modes)]
    for d in range(1, n_row):
        peer = (p + d) % n_row
        to(back_r.at[peer], back_r.at[peer], bs_send.at[d], bs_recv.at[peer], peer, q).wait_recv()
        total = total + back_r[peer]
    back[...] = total

    for d in range(1, n_col):
        img_copy(d).wait_send()
    for d in range(1, n_row):
        back_copy(d).wait_send()
        w_copy(d).wait_send()

    @pl.when(p == owner)
    def _():
        for d in range(1, n_row):
            y_copy(d).wait_send()

    @pl.when(p < 2)
    def _():
        for d in range(1, n_row):
            for kind in range(2):
                small_copy(kind, d).wait_send()

    def drain_sib(block, _):
        sib(block, core).wait_send()
        return 0

    lax.fori_loop(0, rows + 1, drain_sib, 0)

    def drain(low, high, stop):
        @pl.when(pos != stop)
        def _():
            def one(block, _):
                ring(block, after).wait_send()
                return 0

            lax.fori_loop(low, high, one, 0)

    drain(0, half, chips - 1)
    drain(half, rows, 1)
    drain(rows, rows + 1, chips - 1)
    for k in range(2):
        @pl.when((p >= k) & (p + 1 < n_row))
        def _(k=k):
            def one(c, _):
                row_copy(k, c, True).wait_send()
                return 0

            lax.fori_loop(0, cols, one, 0)

    @pl.when(p == 1)
    def _():
        def one(c, _):
            row_copy(1, c, False).wait_send()
            return 0

        lax.fori_loop(0, cols, one, 0)


def dot3_split(a, bh, bl):
    ah, al = split(a)
    return mul(ah, bh, NN) + mul(ah, bl, NN) + mul(al, bh, NN)


def update_kernel(
    n_row, tile, fill, fcol, upper, y_in, z_in, img_in, back_in, trace,
    out, y_out, z_out, image, back, uh, ul,
):
    step = pl.program_id(0)
    p = lax.axis_index("row")
    q = lax.axis_index("col")
    cols, width = trace.shape[1], trace.shape[2]

    @pl.when(step == 0)
    def _():
        for k in range(2):
            for c in range(cols):
                high, low = split(upper[k, c])
                uh[k * width:(k + 1) * width, c * width:(c + 1) * width] = high
                ul[k * width:(k + 1) * width, c * width:(c + 1) * width] = low
        y_out[...] = y_in[...]
        z_out[...] = z_in[...]
        for m in range(img_in.shape[0]):
            image[:, m, :] = img_in[m]
        for m in range(back_in.shape[0]):
            back[:, m, :] = back_in[m]

    for t in range(tile):
        a = step * tile + t
        index = a * n_row + p
        l0h, l0l = split(fcol[0, t] * jnp.where(index > 0, 1.0, 0.0))
        l1h, l1l = split(fcol[1, t] * jnp.where(index > 1, 1.0, 0.0))
        lh = jnp.concatenate([l0h, l1h], axis=1)
        ll = jnp.concatenate([l0l, l1l], axis=1)
        for c in range(0, cols, 2):
            bh = uh[:, c * width:(c + 2) * width]
            bl = ul[:, c * width:(c + 2) * width]
            change = mul(lh, bh, NN) + mul(lh, bl, NN) + mul(ll, bh, NN)
            for e in range(2):
                value = trace[t, c + e] * fill[a, c + e].astype(F32) - change[:, e * width:(e + 1) * width]
                if c + e == 0:
                    value = jnp.where(q == 0, fcol[0, t], jnp.where(q == 1, fcol[1, t], value))
                out[t, c + e] = value


def shards(trace, fill, pivots, direct_rhs, adjoint_rhs):
    n_row, n_col = lax.axis_size("row"), lax.axis_size("col")
    rows, cols, width = trace.shape[0], trace.shape[2], trace.shape[4]
    modes = direct_rhs.shape[2]
    blocks = trace.reshape(rows, cols, width, width)
    flags = fill.reshape(rows, cols)
    direct_rhs, adjoint_rhs = direct_rhs[:, 0], adjoint_rhs[:, 0]
    tiles = pivots.reshape(-1, modes, width)
    tiles = jnp.pad(tiles, ((0, max(0, rows - tiles.shape[0])), (0, 0), (0, 0)))
    packed = jnp.stack([direct_rhs, adjoint_rhs, tiles])
    mi, mb = modes // n_col, modes // n_row
    vmem = pl.BlockSpec(memory_space=pltpu.VMEM)
    smem = pl.BlockSpec(memory_space=pltpu.SMEM)
    shape = jax.ShapeDtypeStruct
    dma = pltpu.SemaphoreType.DMA
    fcol, upper, y, z, image, back = pl.pallas_call(
        functools.partial(comm_kernel, n_row, n_col),
        out_shape=(
            shape((2, rows, width, width), F32),
            shape((2, cols, width, width), F32),
            shape((rows, modes, width), F32),
            shape((rows, modes, width), F32),
            shape((mi, rows, width), F32),
            shape((mb, cols, width), F32),
        ),
        in_specs=[smem, vmem, vmem],
        out_specs=[vmem] * 6,
        scratch_shapes=[
            pltpu.VMEM((2, rows + 1, width, width), F32),
            pltpu.VMEM((2, cols, width, width), F32),
            pltpu.VMEM((2, 2, modes, width), F32),
            pltpu.VMEM((2, modes, width), F32),
            pltpu.VMEM((n_row, 2, modes, width), F32),
            pltpu.VMEM((cols, modes, width), F32),
            pltpu.VMEM((cols, 2 * modes, width), BF16),
            pltpu.VMEM((8, width), F32),
            pltpu.VMEM((rows, modes, width), F32),
            pltpu.VMEM((modes, rows, width), F32),
            pltpu.VMEM((n_col, mi, rows, width), F32),
            pltpu.VMEM((cols, modes, width), F32),
            pltpu.VMEM((modes, cols, width), F32),
            pltpu.VMEM((n_row, mb, cols, width), F32),
            dma((2, n_row)), dma((2, 2)),
            dma((rows + 1,)), dma((rows + 1,)), dma((rows + 1,)), dma((rows + 1,)),
            dma((2, cols)), dma((2, cols)), dma((2, cols)),
            dma((n_row,)), dma((n_row,)), dma((n_row,)), dma,
            dma((n_col,)), dma((n_col,)), dma((n_row,)), dma((n_row,)),
        ],
        compiler_params=pltpu.CompilerParams(
            collective_id=0, has_side_effects=True, vmem_limit_bytes=40 * 1024 * 1024
        ),
    )(flags, packed, blocks)

    tile = 4
    whole = lambda x: pl.BlockSpec(x.shape, lambda i: (0,) * x.ndim)
    outs = (
        shape(blocks.shape, F32),
        shape(y.shape, F32),
        shape(z.shape, F32),
        shape((rows, mi, width), F32),
        shape((cols, mb, width), F32),
    )
    factored, direct, adjoint, image, back = pl.pallas_call(
        functools.partial(update_kernel, n_row, tile),
        out_shape=outs,
        grid=(rows // tile,),
        in_specs=[
            smem,
            pl.BlockSpec((2, tile, width, width), lambda i: (0, i, 0, 0)),
            whole(upper), whole(y), whole(z), whole(image), whole(back),
            pl.BlockSpec((tile, cols, width, width), lambda i: (i, 0, 0, 0)),
        ],
        out_specs=[pl.BlockSpec((tile, cols, width, width), lambda i: (i, 0, 0, 0))]
        + [whole(x) for x in outs[1:]],
        scratch_shapes=[
            pltpu.VMEM((2 * width, cols * width), BF16),
            pltpu.VMEM((2 * width, cols * width), BF16),
        ],
        compiler_params=pltpu.CompilerParams(vmem_limit_bytes=32 * 1024 * 1024),
    )(flags, fcol, upper, y, z, image, back, blocks)
    return (
        factored[:, None, :, None],
        direct[:, None],
        adjoint[:, None],
        image[:, None],
        back[:, None],
    )


def solution(mesh):
    placed = (
        P(None, "row", None, "col", None, None),
        P(None, "row", None, "col"),
        P(),
        P(None, "row", None, None),
        P(None, "row", None, None),
    )
    return jax.shard_map(
        shards,
        mesh=mesh,
        in_specs=placed,
        out_specs=(
            P(None, "row", None, "col", None, None),
            P(None, "row", None, None),
            P(None, "row", None, None),
            P(None, "row", "col", None),
            P(None, "col", "row", None),
        ),
        check_vma=False,
    )
```
